32 devices in a mesh: group: 2 (over x), seq: 16 (over z, y, core).
Axes of the slice: x: 2, y: 2, z: 4, core: 2. Of those that a mesh axis runs over, the one named last changes fastest.
Arguments:
- query_rows: bfloat16 [8192, 1536], P(('group', 'seq')), parts along dimension 0, may hold values from -120 to 120
- key_rows: bfloat16 [8192, 1536], P(('group', 'seq')), parts along dimension 0, may hold values from -6.6 to 6.6
- value_rows: bfloat16 [8192, 1536], P(('group', 'seq')), parts along dimension 0, may hold values from -60 to 60
- block_list: int32 [64, 27], P(('group', 'seq')), parts along dimension 0, may hold values from -1 to 31, as said below
- out_weight: bfloat16 [1536, 3072], P('seq'), may hold values from -4 to 4
Outputs:
- projected: bfloat16 [8192, 3072], P(('group', 'seq')), parts along dimension 0
The draws below stay inside these ranges and needn't reach their ends.
There are 2 independent parts, one for each index of `group`. The reference program is written for one: setup_inputs(seed, part) draws one part's arguments, and reference() takes and returns one part's arrays. A program takes and returns all parts, laid end to end along the dimension named above; an argument that names none is the same for every part. Nothing has to cross between parts.
Inputs may be any that keep to these rules, and one draw needn't show every extreme that they name: `block_list`: tile t lies at grid row (t // 2) // 8, grid column (t // 2) % 8 and frame group t % 2. Row t lists distinct key tiles whose grid row, grid column and frame group each differ from t's by at most one; every such tile that shares t's grid row or grid column is listed, t itself among them; the other slots hold -1.
All inputs are finite; a program needn't handle non-finite values.
Results may differ from the reference program's by a relative error of at most 0.0056.
Values may be sent and summed in bfloat16 or wider, within the bound.
A program may use at most 128 MiB of HBM per device.

```python
import jax
import jax.numpy as jnp
from jax import lax

D = 3072
HEADS = 12
HD = 128
TILE = 128
FRAMES = 2
GRID_COLS = 8
TILES = 32
TOKENS = 4096
NB = 27


def key_table(key):
    base = jnp.clip(jax.random.normal(jax.random.fold_in(key, 11), (TOKENS, HEADS * HD), jnp.float32), -6.0, 6.0)
    return base


def draw_key_rows(key, part):
    return key_table(key).astype(jnp.bfloat16)


def draw_query_rows(key, part):
    base = jnp.clip(jax.random.normal(jax.random.fold_in(key, 12), (TOKENS, HEADS * HD), jnp.float32), -6.0, 6.0)
    return base.astype(jnp.bfloat16)


def draw_value_rows(key, part):
    base = jnp.clip(jax.random.normal(jax.random.fold_in(key, 14), (TOKENS, HEADS * HD), jnp.float32), -6.0, 6.0)
    return base.astype(jnp.bfloat16)


def draw_block_list(key, part):
    tiles = jnp.arange(TILES, dtype=jnp.int32)[:, None]
    slots = jnp.arange(NB, dtype=jnp.int32)[None, :]
    place = tiles // FRAMES
    frame = tiles % FRAMES
    grid_row = place // GRID_COLS
    grid_col = place % GRID_COLS
    rows_total = TILES // (FRAMES * GRID_COLS)
    spatial_slot = slots % 9
    frame_step = slots // 9 - 1
    row_step = spatial_slot // 3 - 1
    col_step = spatial_slot % 3 - 1
    other_row = grid_row + row_step
    other_col = grid_col + col_step
    other_frame = frame + frame_step
    valid = (other_row >= 0) & (other_row < rows_total) & (other_col >= 0) & (other_col < GRID_COLS)
    valid = valid & (other_frame >= 0) & (other_frame < FRAMES)
    coin = jax.random.randint(jax.random.fold_in(key, 16), (TILES, NB), 0, 2)
    keep = (row_step == 0) | (col_step == 0) | (coin == 1)
    listed = (other_row * GRID_COLS + other_col) * FRAMES + other_frame
    return jnp.where(valid & keep, listed, -1).astype(jnp.int32)


def shard_levels(rng, shape, cuts, smallest, largest):
    gain = 1.0
    for dim, blocks in cuts:
        heights = jax.random.uniform(jax.random.fold_in(jax.random.fold_in(rng, 6), dim), (blocks,), jnp.float32, smallest / len(cuts), largest / len(cuts))
        gain = gain * jnp.repeat(jnp.exp(heights), shape[dim] // blocks).reshape((-1,) + (1,) * (len(shape) - 1 - dim))
    return gain


def gaussian(rng, dims, width, bound, cuts=(), kind=jnp.bfloat16):
    level = shard_levels(rng, dims, cuts, -0.22, 0.18) if cuts else 1.0
    entries = jax.random.normal(rng, dims, jnp.float32) * width * level
    return jnp.minimum(jnp.maximum(entries, -bound), bound).astype(kind)


def setup_inputs(seed: int = 0, part: int = 0) -> dict:
    key_of = jax.random.split(jax.random.key(seed), 6)
    own_keys = jax.random.split(jax.random.fold_in(key_of[5], part), 6)
    return {
        "query_rows": draw_query_rows(jax.random.fold_in(jax.random.fold_in(key_of[5], part), 71), part),
        "key_rows": draw_key_rows(jax.random.fold_in(jax.random.fold_in(key_of[5], part), 71), part),
        "value_rows": draw_value_rows(jax.random.fold_in(jax.random.fold_in(key_of[5], part), 71), part),
        "block_list": draw_block_list(jax.random.fold_in(jax.random.fold_in(key_of[5], part), 71), part),
        "out_weight": gaussian(key_of[4], (HEADS * HD, D), 0.7, 4.0, ((0, 16),)),
    }


def reference(query_rows, key_rows, value_rows, block_list, out_weight):
    features = HEADS * HD
    scale = HD ** -0.5
    queries_tiled = query_rows.reshape(TILES, TILE, HEADS, HD)
    keys_tiled = key_rows.reshape(TILES, TILE, HEADS, HD)
    values_tiled = value_rows.reshape(TILES, TILE, HEADS, HD)

    def one_tile(index):
        listed = block_list[index]
        safe = jnp.maximum(listed, 0).astype(jnp.int32)
        keys_here = keys_tiled[safe].reshape(NB * TILE, HEADS, HD).astype(jnp.float32)
        values_here = values_tiled[safe].reshape(NB * TILE, HEADS, HD).astype(jnp.float32)
        live = jnp.repeat(listed >= 0, TILE)
        queries_here = queries_tiled[index].astype(jnp.float32)
        scores = jnp.einsum("qhd,khd->hqk", queries_here, keys_here) * scale
        scores = jnp.where(live[None, None, :], scores, -jnp.inf)
        peak = jnp.max(scores, axis=-1, keepdims=True)
        weights = jnp.exp(scores - peak)
        totals = jnp.sum(weights, axis=-1, keepdims=True)
        probs = lax.optimization_barrier(weights.astype(jnp.bfloat16))
        mixed = jnp.einsum("hqk,khd->qhd", probs.astype(jnp.float32), values_here)
        mixed = mixed / jnp.transpose(totals, (1, 0, 2))
        return mixed.astype(jnp.bfloat16).reshape(TILE, features)

    attention = lax.map(one_tile, jnp.arange(TILES, dtype=jnp.int32)).reshape(TILES * TILE, features)
    return jnp.dot(attention, out_weight, preferred_element_type=jnp.float32).astype(jnp.bfloat16)
```

```python
import functools
import math

import jax
import jax.numpy as jnp
from jax import lax
from jax.experimental import pallas as pl
from jax.experimental.pallas import tpu as pltpu
from jax.sharding import PartitionSpec as P

HD = 128
FRAMES = 2
GRID_COLS = 8
MESH = pl.DeviceIdType.MESH
AHEAD = 2


def plan_of(n):
    rows = n // GRID_COLS
    verticals = 0 if rows <= 1 else (1 if rows == 2 else 2)
    return rows, verticals


def attend(q, keys, values, bias, scale):
    rows = q.shape[0]
    scores = jnp.concatenate(
        [
            lax.dot_general(q, k, (((1,), (1,)), ((), ())), preferred_element_type=jnp.float32)
            for k in keys
        ],
        axis=1,
    )
    scores = (scores.reshape(FRAMES, rows // FRAMES, -1) + bias[:, None, :]).reshape(rows, -1)
    peak = jnp.max(scores, axis=1, keepdims=True)
    weights = jnp.exp2((scores - peak) * (scale * math.log2(math.e)))
    totals = jnp.sum(weights, axis=1, keepdims=True)
    probs = weights.astype(jnp.bfloat16)
    mixed = None
    size = values[0].shape[0]
    for i, v in enumerate(values):
        part = jnp.dot(
            probs[:, i * size : (i + 1) * size], v, preferred_element_type=jnp.float32
        )
        mixed = part if mixed is None else mixed + part
    return (mixed / totals).astype(jnp.bfloat16)


def kernel(n, groups, chunks, gather, *refs):
    if gather:
        (q_ref, k_ref, v_ref, list_ref, w_ref, out_ref, wide_ref, kb, vb, bias_ref,
         vs, vr, hs, hr, zs, zr, ys, yr, xs, xr, cs, cr, local_sem) = refs
    else:
        (q_ref, k_ref, v_ref, list_ref, out_ref, kb, vb, bias_ref, vs, vr, hs, hr) = refs
    me = lax.axis_index("seq")
    mine = lax.axis_index("group")
    rows, verticals = plan_of(n)
    row, col = me // GRID_COLS, me % GRID_COLS
    row_count, features = q_ref.shape
    width = features // chunks
    heads_here = width // HD

    def when(condition):
        if condition is None:
            return lambda f: f()
        return pl.when(condition)

    def both(a, b):
        if a is None:
            return b
        if b is None:
            return a
        return jnp.logical_and(a, b)

    if verticals == 1:
        vertical = [((me + GRID_COLS) % n, None, (me + GRID_COLS) % n, None)]
    elif verticals == 2:
        vertical = [
            (me + GRID_COLS, row < rows - 1, me - GRID_COLS, row > 0),
            (me - GRID_COLS, row > 0, me + GRID_COLS, row < rows - 1),
        ]
    else:
        vertical = []
    has_left, has_right = col > 0, col < GRID_COLS - 1
    sides = [(me + 1, has_right, me - 1, has_left), (me - 1, has_left, me + 1, has_right)]

    def slot(side, e):
        return verticals + side * (1 + verticals) + e

    def columns(g):
        return pl.ds(pl.multiple_of(g * width, width), width)

    def vcopy(d, kv, g):
        src, buf = ((k_ref, kb), (v_ref, vb))[kv]
        return pltpu.make_async_remote_copy(
            src_ref=src.at[:, columns(g)],
            dst_ref=buf.at[d, :, columns(g)],
            send_sem=vs.at[d, kv, g],
            recv_sem=vr.at[d, kv, g],
            device_id=(mine, vertical[d][0]),
            device_id_type=MESH,
        )

    def hcopy(side, e, kv, g):
        src, buf = ((k_ref, kb), (v_ref, vb))[kv]
        source = src.at[:, columns(g)] if e == 0 else buf.at[e - 1, :, columns(g)]
        return pltpu.make_async_remote_copy(
            src_ref=source,
            dst_ref=buf.at[slot(side, e), :, columns(g)],
            send_sem=hs.at[side, e, kv, g],
            recv_sem=hr.at[side, e, kv, g],
            device_id=(mine, sides[side][0]),
            device_id_type=MESH,
        )

    if gather:
        outer_count = n // 4
        outer, middle, core = me // 4, (me // 2) % 2, me % 2
        y_peer = outer * 4 + (1 - middle) * 2 + core
        c_peer = outer * 4 + middle * 2 + (1 - core)
        part = w_ref.shape[1] // groups
        names = [(0, 0)] + [(s, d) for s in range(1, outer_count) for d in (0, 1)]
        index_of = {name: i for i, name in enumerate(names)}

        def where_from(name):
            s, d = name
            return outer - s if d == 0 else outer + s

        def exists(name):
            s, d = name
            if s == 0:
                return None
            return outer >= s if d == 0 else outer + s < outer_count

        def cols_of(g):
            return pl.ds(pl.multiple_of(g * part, 128), part)

        def block(name, other, core_there, g):
            m = 1 - middle if other else middle
            return wide_ref.at[where_from(name) * 4 + m * 2 + core_there, :, cols_of(g)]

        def zcopy(name):
            s, d = name
            to = me + 4 if d == 0 else me - 4
            arrives = index_of[(s + 1, d)]
            source = w_ref.at[:, cols_of(mine)] if s == 0 else block(name, False, core, mine)
            return pltpu.make_async_remote_copy(
                src_ref=source,
                dst_ref=block(name, False, core, mine),
                send_sem=zs.at[arrives],
                recv_sem=zr.at[arrives],
                device_id=(mine, to),
                device_id_type=MESH,
            )

        def ycopy(name):
            i = index_of[name]
            source = w_ref.at[:, cols_of(mine)] if name[0] == 0 else block(name, False, core, mine)
            return pltpu.make_async_remote_copy(
                src_ref=source, dst_ref=block(name, False, core, mine),
                send_sem=ys.at[i], recv_sem=yr.at[i],
                device_id=(mine, y_peer), device_id_type=MESH,
            )

        def xcopy(name, other, step):
            i = index_of[name]
            return pltpu.make_async_remote_copy(
                src_ref=block(name, other, core, mine), dst_ref=block(name, other, core, mine),
                send_sem=xs.at[int(other), i, step - 1], recv_sem=xr.at[int(other), i, step - 1],
                device_id=((mine + step) % groups, me), device_id_type=MESH,
            )

        def ccopy(name, other, step):
            i = index_of[name]
            g = (mine + groups - step) % groups
            if name[0] == 0 and not other:
                source, target = w_ref, wide_ref.at[me]
            else:
                source = target = block(name, other, core, g)
            return pltpu.make_async_remote_copy(
                src_ref=source, dst_ref=target,
                send_sem=cs.at[int(other), i, step], recv_sem=cr.at[int(other), i, step],
                device_id=(mine, c_peer), device_id_type=MESH,
            )

        started = []

        def launch(make, condition):
            started.append((make, condition))
            when(condition())(make().start)

        def can_pass(name):
            s, d = name
            return both(exists(name), outer < outer_count - 1 if d == 0 else outer > 0)

        def spread(name, other):
            ok = functools.partial(exists, name)
            for step in range(1, groups if name[0] > 0 or other else 1):
                launch(functools.partial(xcopy, name, other, step), ok)
            launch(functools.partial(ccopy, name, other, 0), ok)

        def arrived_z(name):
            when(exists(name))(zcopy_recv(name))
            if name[0] + 1 < outer_count:
                launch(functools.partial(zcopy, name), functools.partial(can_pass, name))
            launch(functools.partial(ycopy, name), functools.partial(exists, name))
            spread(name, False)

        def zcopy_recv(name):
            s, d = name
            copy = zcopy((s - 1, d))
            return copy.wait_recv

        def arrived_y(name):
            when(exists(name))(ycopy(name).wait_recv)
            spread(name, True)

        def arrived_x(name, other):
            for step in range(1, groups):
                when(exists(name))(xcopy(name, other, step).wait_recv)
                launch(
                    functools.partial(ccopy, name, other, step), functools.partial(exists, name)
                )

        def start_weights():
            for d in (0, 1):
                index_of[(0, d)] = 0
                if outer_count > 1:
                    launch(
                        functools.partial(zcopy, (0, d)), functools.partial(can_pass, (0, d))
                    )
            launch(functools.partial(ycopy, (0, 0)), lambda: None)
            spread((0, 0), False)

        def weight_slot(t):
            for d in (0, 1):
                if t + 1 < outer_count:
                    arrived_z((t + 1, d))
                if 1 <= t < outer_count:
                    arrived_y((t, d))
                if 2 <= t <= outer_count:
                    arrived_x((t - 1, d), False)
                if 3 <= t <= outer_count + 1:
                    arrived_x((t - 2, d), True)
            if t == 0:
                arrived_y((0, 0))
            if t == 1:
                arrived_x((0, 0), True)

        slots = outer_count + 2

    barrier = pltpu.get_barrier_semaphore()
    partners = []
    for to, sends, source, comes in vertical:
        partners.append(((mine, to), sends))
    for to, sends, source, comes in sides:
        partners.append(((mine, to), sends))
    if gather:
        partners.append(((mine, me + 4), outer < outer_count - 1))
        partners.append(((mine, me - 4), outer > 0))
        partners.append(((mine, y_peer), None))
        partners.append(((mine, c_peer), None))
        for step in range(1, groups):
            partners.append((((mine + step) % groups, me), None))
    for device, condition in partners:
        def greet(device=device):
            pl.semaphore_signal(barrier, inc=1, device_id=device, device_id_type=MESH)
        when(condition)(greet)
    expected = sum(
        1 if condition is None else condition.astype(jnp.int32) for device, condition in partners
    )
    pl.semaphore_wait(barrier, expected)

    def start_chunk(g):
        for kv in (0, 1):
            for d in range(verticals):
                when(vertical[d][1])(vcopy(d, kv, g).start)
        for side in (0, 1):
            for kv in (0, 1):
                when(sides[side][1])(hcopy(side, 0, kv, g).start)

    if gather:
        own_copy = pltpu.make_async_copy(w_ref, wide_ref.at[me], local_sem)
        own_copy.start()
        start_weights()
    for g in range(min(AHEAD, chunks)):
        start_chunk(g)

    for side in (0, 1):
        for e in range(1 + verticals):
            there = sides[side][3]
            if e > 0:
                there = both(there, vertical[e - 1][3])

            def clear(at=slot(side, e)):
                kb[at] = jnp.zeros(kb.shape[1:], kb.dtype)
                vb[at] = jnp.zeros(vb.shape[1:], vb.dtype)
            pl.when(jnp.logical_not(there))(clear)
    for d in range(verticals):
        if vertical[d][3] is not None:
            def clear_v(at=d):
                kb[at] = jnp.zeros(kb.shape[1:], kb.dtype)
                vb[at] = jnp.zeros(vb.shape[1:], vb.dtype)
            pl.when(jnp.logical_not(vertical[d][3]))(clear_v)

    tile_rows = row_count // FRAMES
    half = lax.broadcasted_iota(jnp.int32, (FRAMES, row_count), 1) // tile_rows
    order = [(e, s) for e in range(1 + verticals) for s in (None, 0, 1)]
    pieces = []
    for e, s in order:
        place, there = me, None
        if e > 0:
            place, there = vertical[e - 1][2], vertical[e - 1][3]
        if s is not None:
            place = place - 1 if s == 0 else place + 1
            there = both(there, sides[s][3])
        base = place * FRAMES
        if there is not None:
            base = jnp.where(there, base, -2 * FRAMES)
        pieces.append(half + base)
    ids = jnp.concatenate(pieces, axis=1)
    listed = list_ref[...]
    member = jnp.zeros(ids.shape, jnp.bool_)
    for j in range(listed.shape[1]):
        member = jnp.logical_or(member, ids == listed[:, j : j + 1])
    bias_ref[...] = jnp.where(member, 0.0, -jnp.inf)
    scale = HD ** (-0.5)

    def compute(g):
        def head(j, carry):
            at = pl.ds(pl.multiple_of(g * width + j * HD, HD), HD)

            def pick(own, buf, e, s):
                if s is None:
                    return own[:, at] if e == 0 else buf[e - 1, :, at]
                return buf[slot(s, e), :, at]

            out_ref[:, at] = attend(
                q_ref[:, at],
                [pick(k_ref, kb, e, s) for e, s in order],
                [pick(v_ref, vb, e, s) for e, s in order],
                bias_ref[...],
                scale,
            )
            return carry

        lax.fori_loop(0, heads_here, head, 0)

    def step(g, carry):
        @pl.when(g < chunks)
        def _():
            for d in range(verticals):
                for kv in (0, 1):
                    def relay(d=d, kv=kv):
                        vcopy(d, kv, g).wait_recv()
                        for side in (0, 1):
                            pl.when(sides[side][1])(hcopy(side, d + 1, kv, g).start)
                    when(vertical[d][3])(relay)

        @pl.when(g + AHEAD < chunks)
        def _():
            start_chunk(g + AHEAD)

        if gather:
            for t in range(slots):
                if t <= chunks:
                    pl.when(g == t)(functools.partial(weight_slot, t))

        @pl.when(g > 0)
        def _():
            for e in range(1 + verticals):
                for side in (0, 1):
                    there = sides[side][3]
                    if e > 0:
                        there = both(there, vertical[e - 1][3])
                    for kv in (0, 1):
                        pl.when(there)(hcopy(side, e, kv, g - 1).wait_recv)
            compute(g - 1)

        return carry

    lax.fori_loop(0, chunks + 1, step, 0)
    if gather:
        for t in range(chunks + 1, slots):
            weight_slot(t)

    def drain(g, carry):
        for kv in (0, 1):
            for d in range(verticals):
                when(vertical[d][1])(vcopy(d, kv, g).wait_send)
            for side in (0, 1):
                for e in range(1 + verticals):
                    goes = sides[side][1]
                    if e > 0:
                        goes = both(goes, vertical[e - 1][3])
                    when(goes)(hcopy(side, e, kv, g).wait_send)
        return carry

    lax.fori_loop(0, chunks, drain, 0)
    if gather:
        for name in names:
            for other in (False, True):
                for s in range(groups if name[0] > 0 or other else 1):
                    when(exists(name))(ccopy(name, other, s).wait_recv)
        for make, condition in started:
            when(condition())(make().wait_send)
        own_copy.wait()


def body(mesh, query_rows, key_rows, value_rows, block_list, out_weight):
    n, groups = mesh.shape["seq"], mesh.shape["group"]
    row_count, features = query_rows.shape
    head_count = features // HD
    chunks = head_count // math.gcd(head_count, 2)
    rows, verticals = plan_of(n)
    depth, model = out_weight.shape
    outer = n // 4
    gather = n % 4 == 0 and outer <= 4 and model % (128 * groups) == 0
    slots = 2 * (1 + verticals) + verticals
    vmem = pl.BlockSpec(memory_space=pltpu.VMEM)
    dma = pltpu.SemaphoreType.DMA
    blocks = 3 * (1 + verticals)
    args = [query_rows, key_rows, value_rows, block_list]
    out_shape = [jax.ShapeDtypeStruct((row_count, features), jnp.bfloat16)]
    out_specs = [vmem]
    scratch = [
        pltpu.VMEM((slots, row_count, features), jnp.bfloat16),
        pltpu.VMEM((slots, row_count, features), jnp.bfloat16),
        pltpu.VMEM((FRAMES, blocks * row_count), jnp.float32),
        dma((max(verticals, 1), 2, chunks)),
        dma((max(verticals, 1), 2, chunks)),
        dma((2, 1 + verticals, 2, chunks)),
        dma((2, 1 + verticals, 2, chunks)),
    ]
    if gather:
        count = 2 * outer - 1
        args.append(out_weight)
        out_shape.append(jax.ShapeDtypeStruct((n, depth, model), jnp.bfloat16))
        out_specs.append(pl.BlockSpec(memory_space=pl.ANY))
        scratch += [
            dma((count,)), dma((count,)),
            dma((count,)), dma((count,)),
            dma((2, count, max(groups - 1, 1))), dma((2, count, max(groups - 1, 1))),
            dma((2, count, groups)), dma((2, count, groups)),
            dma,
        ]
    results = pl.pallas_call(
        functools.partial(kernel, n, groups, chunks, gather),
        out_shape=out_shape,
        in_specs=[vmem] * len(args),
        out_specs=out_specs,
        scratch_shapes=scratch,
        compiler_params=pltpu.CompilerParams(collective_id=0, has_side_effects=True),
    )(*args)
    if gather:
        attention, wide = results
        wide = wide.reshape(n * depth, model)
    else:
        (attention,) = results
        wide = lax.all_gather(out_weight, "seq", axis=0, tiled=True)
    return jnp.dot(attention, wide, preferred_element_type=jnp.float32).astype(jnp.bfloat16)


def solution(mesh):
    placed = (
        P(("group", "seq"), None),
        P(("group", "seq"), None),
        P(("group", "seq"), None),
        P(("group", "seq"), None),
        P("seq", None),
    )
    return jax.shard_map(
        functools.partial(body, mesh),
        mesh=mesh,
        in_specs=placed,
        out_specs=P(("group", "seq"), None),
        check_vma=False,
    )
```

```python
import functools
import math

import jax
import jax.numpy as jnp
from jax import lax
from jax.experimental import pallas as pl
from jax.experimental.pallas import tpu as pltpu
from jax.sharding import PartitionSpec as P

HD = 128
FRAMES = 2
GRID_COLS = 8
MESH = pl.DeviceIdType.MESH
AHEAD = 1
Z_AT, Y_AT, XZ_AT, XY_AT = (0, 2), (2, 2), (3, 2), (5, 2)
Y_OWN, XY_OWN = 1, 4


def plan_of(n):
    rows = n // GRID_COLS
    verticals = 0 if rows <= 1 else (1 if rows == 2 else 2)
    return rows, verticals


def attend(q, keys, values, bias, scale):
    rows = q.shape[0]
    scores = jnp.concatenate(
        [
            lax.dot_general(q, k, (((1,), (1,)), ((), ())), preferred_element_type=jnp.float32)
            for k in keys
        ],
        axis=1,
    )
    scores = (scores.reshape(FRAMES, rows // FRAMES, -1) + bias[:, None, :]).reshape(rows, -1)
    peak = jnp.max(scores, axis=1, keepdims=True)
    weights = jnp.exp2((scores - peak) * (scale * math.log2(math.e)))
    totals = jnp.sum(weights, axis=1, keepdims=True)
    probs = weights.astype(jnp.bfloat16)
    mixed = None
    size = values[0].shape[0]
    for i, v in enumerate(values):
        part = jnp.dot(
            probs[:, i * size : (i + 1) * size], v, preferred_element_type=jnp.float32
        )
        mixed = part if mixed is None else mixed + part
    return (mixed / totals).astype(jnp.bfloat16)


def kernel(n, groups, chunks, gather, *refs):
    if gather:
        (q_ref, k_ref, v_ref, list_ref, w_ref, out_ref, wide_ref, kb, vb, bias_ref,
         vs, vr, hs, hr, zs, zr, ys, yr, xs, xr, cs, cr, local_sem) = refs
    else:
        (q_ref, k_ref, v_ref, list_ref, out_ref, kb, vb, bias_ref, vs, vr, hs, hr) = refs
    me = lax.axis_index("seq")
    mine = lax.axis_index("group")
    rows, verticals = plan_of(n)
    row, col = me // GRID_COLS, me % GRID_COLS
    row_count, features = q_ref.shape
    width = features // chunks
    heads_here = width // HD

    def when(condition):
        if condition is None:
            return lambda f: f()
        return pl.when(condition)

    def both(a, b):
        if a is None:
            return b
        if b is None:
            return a
        return jnp.logical_and(a, b)

    if verticals == 1:
        vertical = [((me + GRID_COLS) % n, None, (me + GRID_COLS) % n, None)]
    elif verticals == 2:
        vertical = [
            (me + GRID_COLS, row < rows - 1, me - GRID_COLS, row > 0),
            (me - GRID_COLS, row > 0, me + GRID_COLS, row < rows - 1),
        ]
    else:
        vertical = []
    has_left, has_right = col > 0, col < GRID_COLS - 1
    sides = [(me + 1, has_right, me - 1, has_left), (me - 1, has_left, me + 1, has_right)]

    def slot(side, e):
        return verticals + side * (1 + verticals) + e

    def columns(g):
        return pl.ds(pl.multiple_of(g * width, width), width)

    def vcopy(d, kv, g):
        src, buf = ((k_ref, kb), (v_ref, vb))[kv]
        return pltpu.make_async_remote_copy(
            src_ref=src.at[:, columns(g)],
            dst_ref=buf.at[d, :, columns(g)],
            send_sem=vs.at[d, kv, g],
            recv_sem=vr.at[d, kv, g],
            device_id=(mine, vertical[d][0]),
            device_id_type=MESH,
        )

    def hcopy(side, e, kv, g):
        src, buf = ((k_ref, kb), (v_ref, vb))[kv]
        source = src.at[:, columns(g)] if e == 0 else buf.at[e - 1, :, columns(g)]
        return pltpu.make_async_remote_copy(
            src_ref=source,
            dst_ref=buf.at[slot(side, e), :, columns(g)],
            send_sem=hs.at[side, e, kv, g],
            recv_sem=hr.at[side, e, kv, g],
            device_id=(mine, sides[side][0]),
            device_id_type=MESH,
        )

    if gather:
        outer_count = n // 4
        outer, middle, core = me // 4, (me // 2) % 2, me % 2
        y_peer = outer * 4 + (1 - middle) * 2 + core
        c_peer = outer * 4 + middle * 2 + (1 - core)
        part = w_ref.shape[1] // groups
        names = [(0, 0)] + [(s, d) for s in range(1, outer_count) for d in (0, 1)]
        index_of = {name: i for i, name in enumerate(names)}

        def where_from(name):
            s, d = name
            return outer - s if d == 0 else outer + s

        def exists(name):
            s, d = name
            if s == 0:
                return None
            return outer >= s if d == 0 else outer + s < outer_count

        def cols_of(g):
            return pl.ds(pl.multiple_of(g * part, 128), part)

        def block(name, other, core_there, g):
            m = 1 - middle if other else middle
            return wide_ref.at[where_from(name) * 4 + m * 2 + core_there, :, cols_of(g)]

        def zcopy(name):
            s, d = name
            to = me + 4 if d == 0 else me - 4
            arrives = index_of[(s + 1, d)]
            source = w_ref.at[:, cols_of(mine)] if s == 0 else block(name, False, core, mine)
            return pltpu.make_async_remote_copy(
                src_ref=source,
                dst_ref=block(name, False, core, mine),
                send_sem=zs.at[arrives],
                recv_sem=zr.at[arrives],
                device_id=(mine, to),
                device_id_type=MESH,
            )

        def ycopy(name):
            i = index_of[name]
            source = w_ref.at[:, cols_of(mine)] if name[0] == 0 else block(name, False, core, mine)
            return pltpu.make_async_remote_copy(
                src_ref=source, dst_ref=block(name, False, core, mine),
                send_sem=ys.at[i], recv_sem=yr.at[i],
                device_id=(mine, y_peer), device_id_type=MESH,
            )

        def xcopy(name, other, step):
            i = index_of[name]
            return pltpu.make_async_remote_copy(
                src_ref=block(name, other, core, mine), dst_ref=block(name, other, core, mine),
                send_sem=xs.at[int(other), i, step - 1], recv_sem=xr.at[int(other), i, step - 1],
                device_id=((mine + step) % groups, me), device_id_type=MESH,
            )

        def ccopy(name, other, step):
            i = index_of[name]
            g = (mine + groups - step) % groups
            if name[0] == 0 and not other:
                source, target = w_ref, wide_ref.at[me]
            else:
                source = target = block(name, other, core, g)
            return pltpu.make_async_remote_copy(
                src_ref=source, dst_ref=target,
                send_sem=cs.at[int(other), i, step], recv_sem=cr.at[int(other), i, step],
                device_id=(mine, c_peer), device_id_type=MESH,
            )

        started = []

        def launch(make, condition):
            started.append((make, condition))
            when(condition())(make().start)

        def can_pass(name):
            s, d = name
            return both(exists(name), outer < outer_count - 1 if d == 0 else outer > 0)

        def spread(name, other):
            ok = functools.partial(exists, name)
            for step in range(1, groups if name[0] > 0 or other else 1):
                launch(functools.partial(xcopy, name, other, step), ok)
            launch(functools.partial(ccopy, name, other, 0), ok)

        def arrived_z(name):
            when(exists(name))(zcopy_recv(name))
            if name[0] + 1 < outer_count:
                launch(functools.partial(zcopy, name), functools.partial(can_pass, name))
            launch(functools.partial(ycopy, name), functools.partial(exists, name))
            spread(name, False)

        def zcopy_recv(name):
            s, d = name
            copy = zcopy((s - 1, d))
            return copy.wait_recv

        def arrived_y(name):
            when(exists(name))(ycopy(name).wait_recv)
            spread(name, True)

        def arrived_x(name, other):
            for step in range(1, groups):
                when(exists(name))(xcopy(name, other, step).wait_recv)
                launch(
                    functools.partial(ccopy, name, other, step), functools.partial(exists, name)
                )

        def start_weights():
            for d in (0, 1):
                index_of[(0, d)] = 0
                if outer_count > 1:
                    launch(
                        functools.partial(zcopy, (0, d)), functools.partial(can_pass, (0, d))
                    )
            launch(functools.partial(ycopy, (0, 0)), lambda: None)
            spread((0, 0), False)

        def weight_slot(t):
            for s, d in names:
                if s > 0 and t == Z_AT[0] + Z_AT[1] * (s - 1):
                    arrived_z((s, d))
            for s, d in names:
                if t == (Y_AT[0] + Y_AT[1] * (s - 1) if s > 0 else Y_OWN):
                    arrived_y((s, d))
            for s, d in names:
                if s > 0 and t == XZ_AT[0] + XZ_AT[1] * (s - 1):
                    arrived_x((s, d), False)
                if t == (XY_AT[0] + XY_AT[1] * (s - 1) if s > 0 else XY_OWN):
                    arrived_x((s, d), True)

        slots = 1 + max(
            a + b * max(outer_count - 2, 0) for a, b in (Z_AT, Y_AT, XZ_AT, XY_AT)
        )
        slots = max(slots, Y_OWN + 1, XY_OWN + 1)

    barrier = pltpu.get_barrier_semaphore()
    partners = []
    for to, sends, source, comes in vertical:
        partners.append(((mine, to), sends))
    for to, sends, source, comes in sides:
        partners.append(((mine, to), sends))
    if gather:
        partners.append(((mine, me + 4), outer < outer_count - 1))
        partners.append(((mine, me - 4), outer > 0))
        partners.append(((mine, y_peer), None))
        partners.append(((mine, c_peer), None))
        for step in range(1, groups):
            partners.append((((mine + step) % groups, me), None))
    for device, condition in partners:
        def greet(device=device):
            pl.semaphore_signal(barrier, inc=1, device_id=device, device_id_type=MESH)
        when(condition)(greet)
    expected = sum(
        1 if condition is None else condition.astype(jnp.int32) for device, condition in partners
    )
    pl.semaphore_wait(barrier, expected)

    def start_chunk(g):
        for kv in (0, 1):
            for d in range(verticals):
                when(vertical[d][1])(vcopy(d, kv, g).start)
        for side in (0, 1):
            for kv in (0, 1):
                when(sides[side][1])(hcopy(side, 0, kv, g).start)

    if gather:
        own_copy = pltpu.make_async_copy(w_ref, wide_ref.at[me], local_sem)
        own_copy.start()
        start_weights()
    for g in range(min(AHEAD, chunks)):
        start_chunk(g)

    for side in (0, 1):
        for e in range(1 + verticals):
            there = sides[side][3]
            if e > 0:
                there = both(there, vertical[e - 1][3])

            def clear(at=slot(side, e)):
                kb[at] = jnp.zeros(kb.shape[1:], kb.dtype)
                vb[at] = jnp.zeros(vb.shape[1:], vb.dtype)
            pl.when(jnp.logical_not(there))(clear)
    for d in range(verticals):
        if vertical[d][3] is not None:
            def clear_v(at=d):
                kb[at] = jnp.zeros(kb.shape[1:], kb.dtype)
                vb[at] = jnp.zeros(vb.shape[1:], vb.dtype)
            pl.when(jnp.logical_not(vertical[d][3]))(clear_v)

    tile_rows = row_count // FRAMES
    half = lax.broadcasted_iota(jnp.int32, (FRAMES, row_count), 1) // tile_rows
    order = [(e, s) for e in range(1 + verticals) for s in (None, 0, 1)]
    pieces = []
    for e, s in order:
        place, there = me, None
        if e > 0:
            place, there = vertical[e - 1][2], vertical[e - 1][3]
        if s is not None:
            place = place - 1 if s == 0 else place + 1
            there = both(there, sides[s][3])
        base = place * FRAMES
        if there is not None:
            base = jnp.where(there, base, -2 * FRAMES)
        pieces.append(half + base)
    ids = jnp.concatenate(pieces, axis=1)
    listed = list_ref[...]
    member = jnp.zeros(ids.shape, jnp.bool_)
    for j in range(listed.shape[1]):
        member = jnp.logical_or(member, ids == listed[:, j : j + 1])
    bias_ref[...] = jnp.where(member, 0.0, -jnp.inf)
    scale = HD ** (-0.5)

    def compute(g):
        def head(j, carry):
            at = pl.ds(pl.multiple_of(g * width + j * HD, HD), HD)

            def pick(own, buf, e, s):
                if s is None:
                    return own[:, at] if e == 0 else buf[e - 1, :, at]
                return buf[slot(s, e), :, at]

            out_ref[:, at] = attend(
                q_ref[:, at],
                [pick(k_ref, kb, e, s) for e, s in order],
                [pick(v_ref, vb, e, s) for e, s in order],
                bias_ref[...],
                scale,
            )
            return carry

        lax.fori_loop(0, heads_here, head, 0)

    def step(g, carry):
        @pl.when(g < chunks)
        def _():
            for d in range(verticals):
                for kv in (0, 1):
                    def relay(d=d, kv=kv):
                        vcopy(d, kv, g).wait_recv()
                        for side in (0, 1):
                            pl.when(sides[side][1])(hcopy(side, d + 1, kv, g).start)
                    when(vertical[d][3])(relay)

        if gather:
            for t in range(slots):
                if t <= chunks:
                    pl.when(g == t)(functools.partial(weight_slot, t))

        @pl.when(g + AHEAD < chunks)
        def _():
            start_chunk(g + AHEAD)

        @pl.when(g > 0)
        def _():
            for e in range(1 + verticals):
                for side in (0, 1):
                    there = sides[side][3]
                    if e > 0:
                        there = both(there, vertical[e - 1][3])
                    for kv in (0, 1):
                        pl.when(there)(hcopy(side, e, kv, g - 1).wait_recv)
            compute(g - 1)

        return carry

    lax.fori_loop(0, chunks + 1, step, 0)
    if gather:
        for t in range(chunks + 1, slots):
            weight_slot(t)

    def drain(g, carry):
        for kv in (0, 1):
            for d in range(verticals):
                when(vertical[d][1])(vcopy(d, kv, g).wait_send)
            for side in (0, 1):
                for e in range(1 + verticals):
                    goes = sides[side][1]
                    if e > 0:
                        goes = both(goes, vertical[e - 1][3])
                    when(goes)(hcopy(side, e, kv, g).wait_send)
        return carry

    lax.fori_loop(0, chunks, drain, 0)
    if gather:
        for name in names:
            for other in (False, True):
                for s in range(groups if name[0] > 0 or other else 1):
                    when(exists(name))(ccopy(name, other, s).wait_recv)
        for make, condition in started:
            when(condition())(make().wait_send)
        own_copy.wait()


def body(mesh, query_rows, key_rows, value_rows, block_list, out_weight):
    n, groups = mesh.shape["seq"], mesh.shape["group"]
    row_count, features = query_rows.shape
    head_count = features // HD
    chunks = head_count
    rows, verticals = plan_of(n)
    depth, model = out_weight.shape
    outer = n // 4
    gather = n % 4 == 0 and outer <= 4 and model % (128 * groups) == 0
    slots = 2 * (1 + verticals) + verticals
    vmem = pl.BlockSpec(memory_space=pltpu.VMEM)
    dma = pltpu.SemaphoreType.DMA
    blocks = 3 * (1 + verticals)
    args = [query_rows, key_rows, value_rows, block_list]
    out_shape = [jax.ShapeDtypeStruct((row_count, features), jnp.bfloat16)]
    out_specs = [vmem]
    scratch = [
        pltpu.VMEM((slots, row_count, features), jnp.bfloat16),
        pltpu.VMEM((slots, row_count, features), jnp.bfloat16),
        pltpu.VMEM((FRAMES, blocks * row_count), jnp.float32),
        dma((max(verticals, 1), 2, chunks)),
        dma((max(verticals, 1), 2, chunks)),
        dma((2, 1 + verticals, 2, chunks)),
        dma((2, 1 + verticals, 2, chunks)),
    ]
    if gather:
        count = 2 * outer - 1
        args.append(out_weight)
        out_shape.append(jax.ShapeDtypeStruct((n, depth, model), jnp.bfloat16))
        out_specs.append(pl.BlockSpec(memory_space=pl.ANY))
        scratch += [
            dma((count,)), dma((count,)),
            dma((count,)), dma((count,)),
            dma((2, count, max(groups - 1, 1))), dma((2, count, max(groups - 1, 1))),
            dma((2, count, groups)), dma((2, count, groups)),
            dma,
        ]
    results = pl.pallas_call(
        functools.partial(kernel, n, groups, chunks, gather),
        out_shape=out_shape,
        in_specs=[vmem] * len(args),
        out_specs=out_specs,
        scratch_shapes=scratch,
        compiler_params=pltpu.CompilerParams(collective_id=0, has_side_effects=True),
    )(*args)
    if gather:
        attention, wide = results
        wide = wide.reshape(n * depth, model)
    else:
        (attention,) = results
        wide = lax.all_gather(out_weight, "seq", axis=0, tiled=True)
    return jnp.dot(attention, wide, preferred_element_type=jnp.float32).astype(jnp.bfloat16)


def solution(mesh):
    placed = (
        P(("group", "seq"), None),
        P(("group", "seq"), None),
        P(("group", "seq"), None),
        P(("group", "seq"), None),
        P("seq", None),
    )
    return jax.shard_map(
        functools.partial(body, mesh),
        mesh=mesh,
        in_specs=placed,
        out_specs=P(("group", "seq"), None),
        check_vma=False,
    )
```

```python
import functools
import math

import jax
import jax.numpy as jnp
from jax import lax
from jax.experimental import pallas as pl
from jax.experimental.pallas import tpu as pltpu
from jax.sharding import PartitionSpec as P

HD = 128
FRAMES = 2
GRID_COLS = 8
MESH = pl.DeviceIdType.MESH
AHEAD = 1
Z_AT, Y_AT, XZ_AT, XY_AT = (0, 2), (2, 2), (3, 2), (5, 2)
Y_OWN, XY_OWN = 1, 4


def plan_of(n):
    rows = n // GRID_COLS
    verticals = 0 if rows <= 1 else (1 if rows == 2 else 2)
    return rows, verticals


def attend(q, keys, values, bias, scale):
    rows = q.shape[0]
    scores = jnp.concatenate(
        [
            lax.dot_general(q, k, (((1,), (1,)), ((), ())), preferred_element_type=jnp.float32)
            for k in keys
        ],
        axis=1,
    )
    scores = (scores.reshape(FRAMES, rows // FRAMES, -1) + bias[:, None, :]).reshape(rows, -1)
    peak = jnp.max(scores, axis=1, keepdims=True)
    weights = jnp.exp2((scores - peak) * (scale * math.log2(math.e)))
    totals = jnp.sum(weights, axis=1, keepdims=True)
    probs = weights.astype(jnp.bfloat16)
    mixed = None
    size = values[0].shape[0]
    for i, v in enumerate(values):
        part = jnp.dot(
            probs[:, i * size : (i + 1) * size], v, preferred_element_type=jnp.float32
        )
        mixed = part if mixed is None else mixed + part
    return (mixed / totals).astype(jnp.bfloat16)


def kernel(n, groups, chunks, gather, *refs):
    if gather:
        (q_ref, k_ref, v_ref, list_ref, w_ref, out_ref, wide_ref, kb, vb, bias_ref,
         vs, vr, hs, hr, zs, zr, ys, yr, xs, xr, cs, cr, local_sem) = refs
    else:
        (q_ref, k_ref, v_ref, list_ref, out_ref, kb, vb, bias_ref, vs, vr, hs, hr) = refs
    me = lax.axis_index("seq")
    mine = lax.axis_index("group")
    rows, verticals = plan_of(n)
    row, col = me // GRID_COLS, me % GRID_COLS
    row_count, features = q_ref.shape
    width = features // chunks
    heads_here = width // HD

    def when(condition):
        if condition is None:
            return lambda f: f()
        return pl.when(condition)

    def both(a, b):
        if a is None:
            return b
        if b is None:
            return a
        return jnp.logical_and(a, b)

    if verticals == 1:
        vertical = [((me + GRID_COLS) % n, None, (me + GRID_COLS) % n, None)]
    elif verticals == 2:
        vertical = [
            (me + GRID_COLS, row < rows - 1, me - GRID_COLS, row > 0),
            (me - GRID_COLS, row > 0, me + GRID_COLS, row < rows - 1),
        ]
    else:
        vertical = []
    has_left, has_right = col > 0, col < GRID_COLS - 1
    sides = [(me + 1, has_right, me - 1, has_left), (me - 1, has_left, me + 1, has_right)]

    def slot(side, e):
        return verticals + side * (1 + verticals) + e

    def columns(g):
        return pl.ds(pl.multiple_of(g * width, width), width)

    def vcopy(d, kv, g):
        src, buf = ((k_ref, kb), (v_ref, vb))[kv]
        return pltpu.make_async_remote_copy(
            src_ref=src.at[:, columns(g)],
            dst_ref=buf.at[d, :, columns(g)],
            send_sem=vs.at[d, kv, g],
            recv_sem=vr.at[d, kv, g],
            device_id=(mine, vertical[d][0]),
            device_id_type=MESH,
        )

    def hcopy(side, e, kv, g):
        src, buf = ((k_ref, kb), (v_ref, vb))[kv]
        source = src.at[:, columns(g)] if e == 0 else buf.at[e - 1, :, columns(g)]
        return pltpu.make_async_remote_copy(
            src_ref=source,
            dst_ref=buf.at[slot(side, e), :, columns(g)],
            send_sem=hs.at[side, e, kv, g],
            recv_sem=hr.at[side, e, kv, g],
            device_id=(mine, sides[side][0]),
            device_id_type=MESH,
        )

    if gather:
        outer_count = n // 4
        outer, middle, core = me // 4, (me // 2) % 2, me % 2
        y_peer = outer * 4 + (1 - middle) * 2 + core
        c_peer = outer * 4 + middle * 2 + (1 - core)
        part = w_ref.shape[1] // groups
        names = [(0, 0)] + [(s, d) for s in range(1, outer_count) for d in (0, 1)]
        index_of = {name: i for i, name in enumerate(names)}

        def where_from(name):
            s, d = name
            return outer - s if d == 0 else outer + s

        def exists(name):
            s, d = name
            if s == 0:
                return None
            return outer >= s if d == 0 else outer + s < outer_count

        def cols_of(g):
            return pl.ds(pl.multiple_of(g * part, 128), part)

        def block(name, other, core_there, g):
            m = 1 - middle if other else middle
            return wide_ref.at[where_from(name) * 4 + m * 2 + core_there, :, cols_of(g)]

        def zcopy(name):
            s, d = name
            to = me + 4 if d == 0 else me - 4
            arrives = index_of[(s + 1, d)]
            source = w_ref.at[:, cols_of(mine)] if s == 0 else block(name, False, core, mine)
            return pltpu.make_async_remote_copy(
                src_ref=source,
                dst_ref=block(name, False, core, mine),
                send_sem=zs.at[arrives],
                recv_sem=zr.at[arrives],
                device_id=(mine, to),
                device_id_type=MESH,
            )

        def ycopy(name):
            i = index_of[name]
            source = w_ref.at[:, cols_of(mine)] if name[0] == 0 else block(name, False, core, mine)
            return pltpu.make_async_remote_copy(
                src_ref=source, dst_ref=block(name, False, core, mine),
                send_sem=ys.at[i], recv_sem=yr.at[i],
                device_id=(mine, y_peer), device_id_type=MESH,
            )

        def xcopy(name, other, step):
            i = index_of[name]
            return pltpu.make_async_remote_copy(
                src_ref=block(name, other, core, mine), dst_ref=block(name, other, core, mine),
                send_sem=xs.at[int(other), i, step - 1], recv_sem=xr.at[int(other), i, step - 1],
                device_id=((mine + step) % groups, me), device_id_type=MESH,
            )

        def ccopy(name, other, step):
            i = index_of[name]
            g = (mine + groups - step) % groups
            if name[0] == 0 and not other:
                source, target = w_ref, wide_ref.at[me]
            else:
                source = target = block(name, other, core, g)
            return pltpu.make_async_remote_copy(
                src_ref=source, dst_ref=target,
                send_sem=cs.at[int(other), i, step], recv_sem=cr.at[int(other), i, step],
                device_id=(mine, c_peer), device_id_type=MESH,
            )

        started = []

        def launch(make, condition):
            started.append((make, condition))
            when(condition())(make().start)

        def can_pass(name):
            s, d = name
            return both(exists(name), outer < outer_count - 1 if d == 0 else outer > 0)

        def spread(name, other):
            ok = functools.partial(exists, name)
            for step in range(1, groups if name[0] > 0 or other else 1):
                launch(functools.partial(xcopy, name, other, step), ok)
            launch(functools.partial(ccopy, name, other, 0), ok)

        def arrived_z(name):
            when(exists(name))(zcopy_recv(name))
            if name[0] + 1 < outer_count:
                launch(functools.partial(zcopy, name), functools.partial(can_pass, name))
            launch(functools.partial(ycopy, name), functools.partial(exists, name))
            spread(name, False)

        def zcopy_recv(name):
            s, d = name
            copy = zcopy((s - 1, d))
            return copy.wait_recv

        def arrived_y(name):
            when(exists(name))(ycopy(name).wait_recv)
            spread(name, True)

        def arrived_x(name, other):
            for step in range(1, groups):
                when(exists(name))(xcopy(name, other, step).wait_recv)
                launch(
                    functools.partial(ccopy, name, other, step), functools.partial(exists, name)
                )

        def start_weights():
            for d in (0, 1):
                index_of[(0, d)] = 0
                if outer_count > 1:
                    launch(
                        functools.partial(zcopy, (0, d)), functools.partial(can_pass, (0, d))
                    )
            launch(functools.partial(ycopy, (0, 0)), lambda: None)
            spread((0, 0), False)

        def weight_slot(t):
            for s, d in names:
                if s > 0 and t == Z_AT[0] + Z_AT[1] * (s - 1):
                    arrived_z((s, d))
            for s, d in names:
                if t == (Y_AT[0] + Y_AT[1] * (s - 1) if s > 0 else Y_OWN):
                    arrived_y((s, d))
            for s, d in names:
                if s > 0 and t == XZ_AT[0] + XZ_AT[1] * (s - 1):
                    arrived_x((s, d), False)
                if t == (XY_AT[0] + XY_AT[1] * (s - 1) if s > 0 else XY_OWN):
                    arrived_x((s, d), True)

        slots = 1 + max(
            a + b * max(outer_count - 2, 0) for a, b in (Z_AT, Y_AT, XZ_AT, XY_AT)
        )
        slots = max(slots, Y_OWN + 1, XY_OWN + 1)

    barrier = pltpu.get_barrier_semaphore()
    partners = []
    for to, sends, source, comes in vertical:
        partners.append(((mine, to), sends))
    for to, sends, source, comes in sides:
        partners.append(((mine, to), sends))
    if gather:
        partners.append(((mine, me + 4), outer < outer_count - 1))
        partners.append(((mine, me - 4), outer > 0))
        partners.append(((mine, y_peer), None))
        partners.append(((mine, c_peer), None))
        for step in range(1, groups):
            partners.append((((mine + step) % groups, me), None))
    for device, condition in partners:
        def greet(device=device):
            pl.semaphore_signal(barrier, inc=1, device_id=device, device_id_type=MESH)
        when(condition)(greet)
    expected = sum(
        1 if condition is None else condition.astype(jnp.int32) for device, condition in partners
    )
    pl.semaphore_wait(barrier, expected)

    def start_chunk(g):
        for kv in (0, 1):
            for d in range(verticals):
                when(vertical[d][1])(vcopy(d, kv, g).start)
        for side in (0, 1):
            for kv in (0, 1):
                when(sides[side][1])(hcopy(side, 0, kv, g).start)

    if gather:
        own_copy = pltpu.make_async_copy(w_ref, wide_ref.at[me], local_sem)
        own_copy.start()
        start_weights()
    for g in range(min(AHEAD, chunks)):
        start_chunk(g)

    for side in (0, 1):
        for e in range(1 + verticals):
            there = sides[side][3]
            if e > 0:
                there = both(there, vertical[e - 1][3])

            def clear(at=slot(side, e)):
                kb[at] = jnp.zeros(kb.shape[1:], kb.dtype)
                vb[at] = jnp.zeros(vb.shape[1:], vb.dtype)
            pl.when(jnp.logical_not(there))(clear)
    for d in range(verticals):
        if vertical[d][3] is not None:
            def clear_v(at=d):
                kb[at] = jnp.zeros(kb.shape[1:], kb.dtype)
                vb[at] = jnp.zeros(vb.shape[1:], vb.dtype)
            pl.when(jnp.logical_not(vertical[d][3]))(clear_v)

    tile_rows = row_count // FRAMES
    half = lax.broadcasted_iota(jnp.int32, (FRAMES, row_count), 1) // tile_rows
    order = [(e, s) for e in range(1 + verticals) for s in (None, 0, 1)]
    pieces = []
    for e, s in order:
        place, there = me, None
        if e > 0:
            place, there = vertical[e - 1][2], vertical[e - 1][3]
        if s is not None:
            place = place - 1 if s == 0 else place + 1
            there = both(there, sides[s][3])
        base = place * FRAMES
        if there is not None:
            base = jnp.where(there, base, -2 * FRAMES)
        pieces.append(half + base)
    ids = jnp.concatenate(pieces, axis=1)
    listed = list_ref[...]
    member = jnp.zeros(ids.shape, jnp.bool_)
    for j in range(listed.shape[1]):
        member = jnp.logical_or(member, ids == listed[:, j : j + 1])
    bias_ref[...] = jnp.where(member, 0.0, -jnp.inf)
    scale = HD ** (-0.5)

    def compute(g):
        def head(j, carry):
            at = pl.ds(pl.multiple_of(g * width + j * HD, HD), HD)

            def pick(own, buf, e, s):
                if s is None:
                    return own[:, at] if e == 0 else buf[e - 1, :, at]
                return buf[slot(s, e), :, at]

            out_ref[:, at] = attend(
                q_ref[:, at],
                [pick(k_ref, kb, e, s) for e, s in order],
                [pick(v_ref, vb, e, s) for e, s in order],
                bias_ref[...],
                scale,
            )
            return carry

        lax.fori_loop(0, heads_here, head, 0)

    def step(g, carry):
        if gather:
            for t in range(slots):
                if t <= chunks:
                    pl.when(g == t)(functools.partial(weight_slot, t))

        @pl.when(g < chunks)
        def _():
            for d in range(verticals):
                for kv in (0, 1):
                    def relay(d=d, kv=kv):
                        vcopy(d, kv, g).wait_recv()
                        for side in (0, 1):
                            pl.when(sides[side][1])(hcopy(side, d + 1, kv, g).start)
                    when(vertical[d][3])(relay)

        @pl.when(g + AHEAD < chunks)
        def _():
            start_chunk(g + AHEAD)

        @pl.when(g > 0)
        def _():
            for e in range(1 + verticals):
                for side in (0, 1):
                    there = sides[side][3]
                    if e > 0:
                        there = both(there, vertical[e - 1][3])
                    for kv in (0, 1):
                        pl.when(there)(hcopy(side, e, kv, g - 1).wait_recv)
            compute(g - 1)

        return carry

    lax.fori_loop(0, chunks + 1, step, 0)
    if gather:
        for t in range(chunks + 1, slots):
            weight_slot(t)

    def drain(g, carry):
        for kv in (0, 1):
            for d in range(verticals):
                when(vertical[d][1])(vcopy(d, kv, g).wait_send)
            for side in (0, 1):
                for e in range(1 + verticals):
                    goes = sides[side][1]
                    if e > 0:
                        goes = both(goes, vertical[e - 1][3])
                    when(goes)(hcopy(side, e, kv, g).wait_send)
        return carry

    lax.fori_loop(0, chunks, drain, 0)
    if gather:
        for name in names:
            for other in (False, True):
                for s in range(groups if name[0] > 0 or other else 1):
                    when(exists(name))(ccopy(name, other, s).wait_recv)
        for make, condition in started:
            when(condition())(make().wait_send)
        own_copy.wait()


def body(mesh, query_rows, key_rows, value_rows, block_list, out_weight):
    n, groups = mesh.shape["seq"], mesh.shape["group"]
    row_count, features = query_rows.shape
    head_count = features // HD
    chunks = head_count
    rows, verticals = plan_of(n)
    depth, model = out_weight.shape
    outer = n // 4
    gather = n % 4 == 0 and outer <= 4 and model % (128 * groups) == 0
    slots = 2 * (1 + verticals) + verticals
    vmem = pl.BlockSpec(memory_space=pltpu.VMEM)
    dma = pltpu.SemaphoreType.DMA
    blocks = 3 * (1 + verticals)
    args = [query_rows, key_rows, value_rows, block_list]
    out_shape = [jax.ShapeDtypeStruct((row_count, features), jnp.bfloat16)]
    out_specs = [vmem]
    scratch = [
        pltpu.VMEM((slots, row_count, features), jnp.bfloat16),
        pltpu.VMEM((slots, row_count, features), jnp.bfloat16),
        pltpu.VMEM((FRAMES, blocks * row_count), jnp.float32),
        dma((max(verticals, 1), 2, chunks)),
        dma((max(verticals, 1), 2, chunks)),
        dma((2, 1 + verticals, 2, chunks)),
        dma((2, 1 + verticals, 2, chunks)),
    ]
    if gather:
        count = 2 * outer - 1
        args.append(out_weight)
        out_shape.append(jax.ShapeDtypeStruct((n, depth, model), jnp.bfloat16))
        out_specs.append(pl.BlockSpec(memory_space=pl.ANY))
        scratch += [
            dma((count,)), dma((count,)),
            dma((count,)), dma((count,)),
            dma((2, count, max(groups - 1, 1))), dma((2, count, max(groups - 1, 1))),
            dma((2, count, groups)), dma((2, count, groups)),
            dma,
        ]
    results = pl.pallas_call(
        functools.partial(kernel, n, groups, chunks, gather),
        out_shape=out_shape,
        in_specs=[vmem] * len(args),
        out_specs=out_specs,
        scratch_shapes=scratch,
        compiler_params=pltpu.CompilerParams(collective_id=0, has_side_effects=True),
    )(*args)
    if gather:
        attention, wide = results
        wide = wide.reshape(n * depth, model)
    else:
        (attention,) = results
        wide = lax.all_gather(out_weight, "seq", axis=0, tiled=True)
    return jnp.dot(attention, wide, preferred_element_type=jnp.float32).astype(jnp.bfloat16)


def solution(mesh):
    placed = (
        P(("group", "seq"), None),
        P(("group", "seq"), None),
        P(("group", "seq"), None),
        P(("group", "seq"), None),
        P("seq", None),
    )
    return jax.shard_map(
        functools.partial(body, mesh),
        mesh=mesh,
        in_specs=placed,
        out_specs=P(("group", "seq"), None),
        check_vma=False,
    )
```
